256 devices in a mesh: tm: 128 (over z, y, x_lo, core), space: 2 (over x_hi).
Axes of the slice: x: 4 (x_hi: 2, x_lo: 2; x = x_hi * 2 + x_lo), y: 4, z: 8, core: 2. Of those that a mesh axis runs over, the one named last changes fastest.
Arguments:
- queries: bfloat16 [128, 16, 16, 768], P('tm', 'space'), may hold values from -24 to 24
- keys: bfloat16 [128, 16, 16, 768], P('tm', 'space'), may hold values from -18 to 18
- values: bfloat16 [128, 16, 16, 768], P('tm', 'space'), may hold values from -18 to 18
- temporal_weight: bfloat16 [3, 768, 768], replicated, may hold values from -0.21875 to 0.21875
- temporal_bias: float32 [768], replicated, may hold values from -3 to 3
- spatial_weight: bfloat16 [3, 3, 768, 768], P(None, None, None, 'space'), may hold values from -0.078125 to 0.078125
- spatial_bias: float32 [768], P('space'), may hold values from -3 to 3
- cotangent: bfloat16 [128, 2, 16, 16, 768], P('tm', None, None, None, 'space'), may hold values from -6 to 6
Outputs:
- attended: bfloat16 [128, 16, 16, 768], P('tm', None, None, 'space')
- refined: bfloat16 [128, 2, 16, 16, 768], P('tm', None, None, None, 'space')
- grad_attended: bfloat16 [128, 16, 16, 768], P('tm', None, None, 'space')
The draws below stay inside these ranges and needn't reach their ends.
All inputs are finite; a program needn't handle non-finite values.
Results may differ from the reference program's by a relative error of at most 0.012.
Values may be sent and summed in bfloat16 or wider, within the bound.
No kernel may reach another device: no remote copies, remote signals or barrier semaphores. Data moves between devices by JAX's collectives and lax.ppermute only.
A program may use at most 128 MiB of HBM per device.

```python
import math
import jax
import jax.numpy as jnp
from jax import lax

HEADS = 12
HEAD = 64
WIDTH = 768
VIDEOS = 2
COLS = 16
ROWS = 16
CLIPS = 128
FRAMES = 64


def base_field(seed_key, salt, shape):
    sub_key = jax.random.fold_in(seed_key, salt)
    return jnp.clip(jax.random.normal(sub_key, shape, jnp.float32), -6.0, 6.0)


def key_field(seed_key):
    shape = (CLIPS, ROWS, COLS, WIDTH)
    field = base_field(seed_key, 101, shape)
    return field


def draw_keys(key, part):
    return key_field(key).astype(jnp.bfloat16)


def draw_queries(key, part):
    shape = (CLIPS, ROWS, COLS, WIDTH)
    field = base_field(key, 202, shape)
    return field.astype(jnp.bfloat16)


def draw_values(key, part):
    level = base_field(key, 303, (CLIPS, 1, 1, WIDTH)) * 2.0
    noise = base_field(key, 304, (CLIPS, ROWS, COLS, WIDTH))
    return (level + noise).astype(jnp.bfloat16)


def block_levels(key, shape, split, smallest, largest):
    loudness, own = 1.0, jax.random.fold_in(key, 6)
    for position, shards_of in split:
        heights = jnp.exp(jax.random.uniform(jax.random.fold_in(own, position), (shards_of,), jnp.float32, smallest / len(split), largest / len(split)))
        loudness = loudness * jnp.repeat(heights, shape[position] // shards_of).reshape([-1 if axis == position else 1 for axis in range(len(shape))])
    return loudness


def bell_draw(own_key, shape, deviation, most, pieces=(), held_as=jnp.bfloat16):
    loudness = block_levels(own_key, shape, pieces, -0.22, 0.18) if pieces else 1.0
    array = jax.random.normal(own_key, shape, jnp.float32) * deviation * loudness
    return jnp.minimum(jnp.maximum(array, -most), most).astype(held_as)


def setup_inputs(seed: int = 0) -> dict:
    streams_of = jax.random.split(jax.random.key(seed), 9)
    return {
        "queries": draw_queries(jax.random.fold_in(streams_of[8], 71), 0),
        "keys": draw_keys(jax.random.fold_in(streams_of[8], 71), 0),
        "values": draw_values(jax.random.fold_in(streams_of[8], 71), 0),
        "temporal_weight": bell_draw(streams_of[3], (3, WIDTH, WIDTH), WIDTH ** -0.5, 0.21875),
        "temporal_bias": bell_draw(streams_of[4], (WIDTH,), 0.5, 3.0, (), jnp.float32),
        "spatial_weight": bell_draw(streams_of[5], (3, 3, WIDTH, WIDTH), (9 * WIDTH) ** -0.5, 0.078125, ((3, 2),)),
        "spatial_bias": bell_draw(streams_of[6], (WIDTH,), 0.5, 3.0, ((0, 2),), jnp.float32),
        "cotangent": bell_draw(streams_of[7], (CLIPS, 2, ROWS, COLS, WIDTH), 1.0, 6.0, ((0, 128), (4, 2))),
    }


def attend_video(video_queries, video_keys, video_values):
    count = FRAMES * ROWS * COLS
    keys_split = video_keys.reshape(count, HEADS, HEAD).astype(jnp.float32)
    values_split = video_values.reshape(count, HEADS, HEAD).astype(jnp.float32)
    query_frames = video_queries.reshape(FRAMES, ROWS * COLS, HEADS, HEAD)
    score_scale = 1.0 / math.sqrt(HEAD)

    def one_frame(frame_queries):
        scores = jnp.einsum('qhd,khd->hqk', frame_queries.astype(jnp.float32), keys_split) * score_scale
        row_max = lax.optimization_barrier(jnp.max(scores, axis=-1, keepdims=True))
        exps = jnp.exp(scores - row_max)
        row_total = lax.optimization_barrier(jnp.sum(exps, axis=-1))
        weights_low = lax.optimization_barrier(exps.astype(jnp.bfloat16)).astype(jnp.float32)
        frame_out = jnp.einsum('hqk,khd->qhd', weights_low, values_split) / jnp.transpose(row_total)[:, :, None]
        return frame_out.reshape(ROWS * COLS, WIDTH).astype(jnp.bfloat16)
    return lax.map(one_frame, query_frames).reshape(FRAMES, ROWS, COLS, WIDTH)

def matmul_rows(left, right):
    product = jnp.dot(left.reshape(-1, left.shape[-1]), right, preferred_element_type=jnp.float32)
    return product.reshape(left.shape[:-1] + (right.shape[1],))

def reference(queries, keys, values, temporal_weight, temporal_bias, spatial_weight, spatial_bias, cotangent):
    per_video = [attend_video(queries[video::VIDEOS], keys[video::VIDEOS], values[video::VIDEOS]) for video in range(VIDEOS)]
    attended = jnp.stack(per_video, axis=1).reshape(CLIPS, ROWS, COLS, WIDTH)
    next_frames = jnp.concatenate([attended[VIDEOS:], jnp.zeros((VIDEOS, ROWS, COLS, WIDTH), jnp.bfloat16)], axis=0)
    even_frames = matmul_rows(attended, temporal_weight[1]) + temporal_bias
    odd_frames = matmul_rows(attended, temporal_weight[2]) + matmul_rows(next_frames, temporal_weight[0]) + temporal_bias
    upsampled = jnp.stack([even_frames, odd_frames], axis=1).astype(jnp.bfloat16)
    padded_up = jnp.pad(upsampled, ((0, 0), (0, 0), (1, 1), (1, 1), (0, 0)))
    refined = jnp.zeros((CLIPS, 2, ROWS, COLS, WIDTH), jnp.float32)
    for row_tap in range(3):
        for col_tap in range(3):
            window = padded_up[:, :, row_tap:row_tap + ROWS, col_tap:col_tap + COLS, :]
            refined = refined + matmul_rows(window, spatial_weight[row_tap, col_tap])
    refined = (refined + spatial_bias).astype(jnp.bfloat16)
    padded_cot = jnp.pad(cotangent, ((0, 0), (0, 0), (1, 1), (1, 1), (0, 0)))
    grad_upsampled = jnp.zeros((CLIPS, 2, ROWS, COLS, WIDTH), jnp.float32)
    for row_tap in range(3):
        for col_tap in range(3):
            window = padded_cot[:, :, 2 - row_tap:2 - row_tap + ROWS, 2 - col_tap:2 - col_tap + COLS, :]
            grad_upsampled = grad_upsampled + matmul_rows(window, jnp.transpose(spatial_weight[row_tap, col_tap]))
    grad_upsampled = grad_upsampled.astype(jnp.bfloat16)
    second_grad = grad_upsampled[:, 1]
    earlier_grad = jnp.concatenate([jnp.zeros((VIDEOS, ROWS, COLS, WIDTH), jnp.bfloat16), second_grad[:-VIDEOS]], axis=0)
    grad_attended = matmul_rows(grad_upsampled[:, 0], jnp.transpose(temporal_weight[1]))
    grad_attended = grad_attended + matmul_rows(second_grad, jnp.transpose(temporal_weight[2]))
    grad_attended = grad_attended + matmul_rows(earlier_grad, jnp.transpose(temporal_weight[0]))
    return (attended, refined, grad_attended.astype(jnp.bfloat16))
```

```python
import functools
import math

import jax
import jax.numpy as jnp
from jax import lax
from jax.experimental import pallas as pl
from jax.experimental.pallas import tpu as pltpu
from jax.sharding import PartitionSpec as P


HEAD = 64
NZ, NY = 8, 4
AX = ("tm", "space")
LOG_SCALE = math.log2(math.e) / 8.0
TINY = 2.0**-60
GROUP = 192
TOK = 128
F32 = jnp.float32
BF16 = jnp.bfloat16
VM = pl.BlockSpec(memory_space=pltpu.MemorySpace.VMEM)
SM = pl.BlockSpec(memory_space=pltpu.MemorySpace.SMEM)
TN = (((0,), (0,)), ((), ()))
NN = (((1,), (0,)), ((), ()))
NT = (((1,), (1,)), ((), ()))


def dot(a, b, dims):
    return lax.dot_general(a, b, dims, preferred_element_type=F32)


def linear(zy, x, core):
    return ((zy * 2 + (x & 1)) * 2 + core) * 2 + (x >> 1)


def pairs(move):
    out = []
    for zy in range(NZ * NY):
        for x in range(4):
            target = move(zy, x)
            if target is None or not 0 <= target[0] < NZ * NY:
                continue
            for core in range(2):
                out.append((linear(zy, x, core), linear(*target, core)))
    return out


def flip_x(bits):
    return pairs(lambda zy, x: (zy, x ^ bits))


def turn_y(by):
    return pairs(lambda zy, x: (zy // NY * NY + (zy + by) % NY, x))


def turn_z(by):
    return pairs(lambda zy, x: ((zy + by * NY) % (NZ * NY), x))


def to_earlier_frame(bits):
    return pairs(lambda zy, x: (zy - ((x ^ bits) & 1), x ^ bits))


def to_next_frame(bits):
    return pairs(lambda zy, x: (zy + (x & 1), x ^ 1 ^ bits))


def send(value, route):
    return lax.ppermute(value, AX, route)


def call(body, outs, in_specs, scratch=(), **kw):
    multi = isinstance(outs, (tuple, list))
    return pl.pallas_call(
        body,
        out_shape=outs,
        in_specs=in_specs,
        out_specs=[VM] * len(outs) if multi else VM,
        scratch_shapes=list(scratch),
        **kw,
    )


def shape(dims, dtype):
    return jax.ShapeDtypeStruct(dims, dtype)


def pack_body(idx, q, k, v, o0, o1, o2, o3, buf):
    for t, ref in enumerate((q, k, v)):
        buf[t] = ref[...].T
    for r, out in enumerate((o0, o1, o2, o3)):
        start = pl.multiple_of(idx[r] * GROUP, 64)
        for t in range(3):
            out[t * GROUP : (t + 1) * GROUP, :] = buf[t, pl.ds(start, GROUP), :]


def unpack_body(idx, p0, p1, p2, p3, q_out, kv_out):
    for r, ref in enumerate((p0, p1, p2, p3)):
        q_out[idx[4 + r]] = ref[:GROUP, :]
        kv_out[r] = ref[GROUP:, :]


def attn_body(*refs, n_kv, first, final):
    qs = refs[:4]
    kvs = refs[4 : 4 + n_kv]
    pos = 4 + n_kv
    if not first:
        acc_in, stat_in = refs[pos : pos + 2]
        pos += 2
    outs = refs[pos:]
    if final:
        o_refs = outs[:4]
        acc_ref, stat_ref = outs[4:6]
    else:
        acc_ref, stat_ref = outs[:2]
    width = 4 * 4 * TOK

    def rows(h, extra=0):
        return slice(extra + h * HEAD, extra + (h + 1) * HEAD)

    def keys(b, h, extra=0):
        parts = [kvs[b][s, rows(h, extra), :] for s in range(kvs[b].shape[0])]
        return jnp.concatenate(parts, axis=1)

    lowest = None
    for h in range(3):
        queries = jnp.concatenate([ref[s, rows(h), :] for ref in qs for s in range(4)], axis=1)
        qf = queries.astype(F32)
        q_norm = jnp.sqrt(jnp.sum(qf * qf, axis=0, keepdims=True))
        k_sq = None
        for b in range(n_kv):
            kf = keys(b, h).astype(F32)
            sq = jnp.max(jnp.sum(kf * kf, axis=0, keepdims=True), axis=1, keepdims=True)
            k_sq = sq if k_sq is None else jnp.maximum(k_sq, sq)
        m = q_norm * (jnp.sqrt(k_sq) * LOG_SCALE)
        if not first:
            m_old = stat_in[4 + h : 5 + h, :]
            m = jnp.maximum(m, m_old)
        acc = total = None
        for b in range(n_kv):
            s = dot(keys(b, h), queries, TN)
            p = jnp.exp2(s * LOG_SCALE - m)
            t = jnp.sum(p, axis=0, keepdims=True)
            o = dot(keys(b, h, GROUP), p.astype(BF16), NN)
            total = t if total is None else total + t
            acc = o if acc is None else acc + o
        if not first:
            fade = jnp.exp2(m_old - m)
            total = total + stat_in[h : h + 1, :] * fade
            acc = acc + acc_in[rows(h), :] * fade
        stat_ref[h : h + 1, :] = total
        stat_ref[4 + h : 5 + h, :] = m
        acc_ref[rows(h), :] = acc
        low = jnp.min(total)
        lowest = low if lowest is None else jnp.minimum(lowest, low)

    @pl.when(jnp.logical_not(lowest >= TINY))
    def _():
        for h in range(3):
            for n, q_ref in enumerate(qs):

                def exact(slot, carry):
                    at = pl.ds(pl.multiple_of((n * 4 + slot) * TOK, TOK), TOK)
                    queries = q_ref[slot, rows(h), :]
                    scores = [dot(keys(b, h), queries, TN) * LOG_SCALE for b in range(n_kv)]
                    m = functools.reduce(
                        jnp.maximum, [jnp.max(s, axis=0, keepdims=True) for s in scores]
                    )
                    if not first:
                        m_old = stat_in[4 + h : 5 + h, at]
                        m = jnp.maximum(m, m_old)
                        fade = jnp.exp2(m_old - m)
                        total = stat_in[h : h + 1, at] * fade
                        acc = acc_in[rows(h), at] * fade
                    else:
                        total = jnp.zeros((1, TOK), F32)
                        acc = jnp.zeros((HEAD, TOK), F32)
                    for b in range(n_kv):
                        p = jnp.exp2(scores[b] - m)
                        total = total + jnp.sum(p, axis=0, keepdims=True)
                        acc = acc + dot(keys(b, h, GROUP), p.astype(BF16), NN)
                    stat_ref[h : h + 1, at] = total
                    stat_ref[4 + h : 5 + h, at] = m
                    acc_ref[rows(h), at] = acc
                    return carry

                lax.fori_loop(0, 4, exact, 0)

    if final:
        for h in range(3):
            total = stat_ref[h : h + 1, :]
            level = stat_ref[4 + h : 5 + h, :] + jnp.log2(total)
            hi = level.astype(BF16)
            mid = (level - hi.astype(F32)).astype(BF16)
            low = (level - hi.astype(F32) - mid.astype(F32)).astype(BF16)
            mean = (acc_ref[rows(h), :] * (1.0 / total)).astype(BF16)
            for n, o_ref in enumerate(o_refs):
                at = slice(n * 4 * TOK, (n + 1) * 4 * TOK)
                o_ref[rows(h), :] = mean[:, at]
                o_ref[GROUP + h * 3 : GROUP + h * 3 + 1, :] = hi[:, at]
                o_ref[GROUP + h * 3 + 1 : GROUP + h * 3 + 2, :] = mid[:, at]
                o_ref[GROUP + h * 3 + 2 : GROUP + h * 3 + 3, :] = low[:, at]
        for o_ref in o_refs:
            o_ref[GROUP + 9 :, :] = jnp.zeros((7, 4 * TOK), BF16)


def attend(qs, kvs, state, final):
    width = 16 * TOK
    body = functools.partial(attn_body, n_kv=len(kvs), first=state is None, final=final)
    args = list(qs) + list(kvs) + ([] if state is None else list(state))
    state_shapes = [((GROUP, width), F32), ((8, width), F32)]
    n_keys = sum(kv.shape[0] for kv in kvs) * TOK
    cost = pl.CostEstimate(
        flops=3 * 2 * 2 * 256 * width * n_keys,
        transcendentals=3 * width * n_keys,
        bytes_accessed=4 << 20,
    )
    if final:
        outs = [shape((GROUP + 16, 4 * TOK), BF16)] * 4
        scratch = [pltpu.VMEM(*s) for s in state_shapes]
    else:
        outs = [shape(*s) for s in state_shapes]
        scratch = []
    return call(body, outs, [VM] * len(args), scratch, cost_estimate=cost, name="attend")(*args)


def merge_body(idx, a0, a1, a2, a3, same, other, buf):
    parts = (a0, a1, a2, a3)
    for h in range(3):
        level = []
        for ref in parts:
            r = GROUP + h * 3
            level.append(
                ref[r : r + 1, :].astype(F32)
                + ref[r + 1 : r + 2, :].astype(F32)
                + ref[r + 2 : r + 3, :].astype(F32)
            )
        top = functools.reduce(jnp.maximum, level)
        weight = [jnp.exp2(v - top) for v in level]
        inv = 1.0 / (weight[0] + weight[1] + weight[2] + weight[3])
        acc = None
        for w, ref in zip(weight, parts):
            t = ref[h * HEAD : (h + 1) * HEAD, :].astype(F32) * (w * inv)
            acc = t if acc is None else acc + t
        acc = acc.astype(BF16)
        for f in range(2):
            buf[f, h * HEAD : (h + 1) * HEAD, :] = acc[:, f * 256 : (f + 1) * 256]
    same[...] = buf[idx[8]]
    other[...] = buf[1 - idx[8]]


def shifted_columns(x, by):
    col = lax.broadcasted_iota(jnp.int32, x.shape, 0) % 16
    if by == 1:
        moved = jnp.concatenate([x[1:], x[:1]], axis=0)
        return jnp.where(col < 15, moved, 0.0)
    moved = jnp.concatenate([x[-1:], x[:-1]], axis=0)
    return jnp.where(col > 0, moved, 0.0)


def fill_windows(win, x):
    c = x.shape[-1]
    for b in range(3):
        y = (x if b == 1 else shifted_columns(x, b - 1)).astype(BF16)
        for s in range(2):
            win[b, s, :16, :] = jnp.zeros((16, c), BF16)
            win[b, s, 272:, :] = jnp.zeros((16, c), BF16)
            win[b, s, 16:272, :] = y[s * 256 : (s + 1) * 256]


def grad_body(idx, cot, sw, tw, a_own, a_peer, b_own, b_peer, win, acc):
    step = pl.program_id(0)

    @pl.when(step == 0)
    def _():
        fill_windows(win, cot[...].astype(F32))
        acc[...] = jnp.zeros_like(acc)

    part = [None, None]
    for b in range(3):
        for s in range(2):
            rows = win[2 - b, s, pl.ds(pl.multiple_of((2 - step) * 16, 16), 256), :]
            t = dot(rows, sw[0, b], NT)
            part[s] = t if part[s] is None else part[s] + t
    for s in range(2):
        acc[s * 256 : (s + 1) * 256, :] += part[s]

    @pl.when(step == 2)
    def _():
        g0 = acc[:256, :].astype(BF16)
        g1 = acc[256:, :].astype(BF16)
        for a_ref, b_ref, half in ((a_own, b_own, idx[9]), (a_peer, b_peer, 1 - idx[9])):
            at = pl.ds(pl.multiple_of(half * 384, 128), 384)
            a_ref[...] = (dot(g0, tw[1, at, :], NT) + dot(g1, tw[2, at, :], NT)).astype(BF16)
            b_ref[...] = dot(g1, tw[0, at, :], NT).astype(BF16)


def gradients(idx, cot, sw, tw):
    out = shape((256, 384), BF16)
    return pl.pallas_call(
        grad_body,
        out_shape=[out] * 4,
        grid=(3,),
        in_specs=[
            SM,
            pl.BlockSpec((512, 384), lambda i: (0, 0)),
            pl.BlockSpec((1, 3, 768, 384), lambda i: (i, 0, 0, 0)),
            pl.BlockSpec((3, 768, 768), lambda i: (0, 0, 0)),
        ],
        out_specs=[pl.BlockSpec((256, 384), lambda i: (0, 0))] * 4,
        scratch_shapes=[pltpu.VMEM((3, 2, 288, 384), BF16), pltpu.VMEM((512, 768), F32)],
        cost_estimate=pl.CostEstimate(
            flops=2 * 512 * 9 * 384 * 768 + 6 * 256 * 768 * 768,
            transcendentals=0,
            bytes_accessed=9 << 20,
        ),
        name="gradients",
    )(idx, cot, sw, tw)


def conv_body(idx, c0, c1, c2, c3, n0, n1, n2, n3, tw, tb, sw, sb, att, refined, cur, nxt, win, acc):
    step = pl.program_id(0)

    @pl.when(step == 0)
    def _():
        for r, (c, n) in enumerate(((c0, n0), (c1, n1), (c2, n2), (c3, n3))):
            at = pl.ds(pl.multiple_of(idx[r] * GROUP, 64), GROUP)
            cur[at, :] = c[...]
            nxt[at, :] = n[...]
        att[...] = cur[pl.ds(pl.multiple_of(idx[9] * 384, 128), 384), :].T
        x = cur[...].T
        y = nxt[...].T
        even = dot(x, tw[1], NN) + tb[...]
        odd = dot(x, tw[2], NN) + dot(y, tw[0], NN) + tb[...]
        up = jnp.concatenate([even, odd], axis=0).astype(BF16)
        fill_windows(win, up.astype(F32))
        acc[...] = jnp.zeros_like(acc) + sb[...]

    part = [None, None]
    for b in range(3):
        for s in range(2):
            rows = win[b, s, pl.ds(pl.multiple_of(step * 16, 16), 256), :]
            t = dot(rows, sw[0, b], NN)
            part[s] = t if part[s] is None else part[s] + t
    for s in range(2):
        acc[s * 256 : (s + 1) * 256, :] += part[s]

    @pl.when(step == 2)
    def _():
        refined[...] = acc[...].astype(BF16)


def convolve(idx, cur, nxt, tw, tb, sw, sb):
    piece = pl.BlockSpec((GROUP, 256), lambda i: (0, 0))
    return pl.pallas_call(
        conv_body,
        out_shape=[shape((256, 384), BF16), shape((512, 384), BF16)],
        grid=(3,),
        in_specs=[SM]
        + [piece] * 8
        + [
            pl.BlockSpec((3, 768, 768), lambda i: (0, 0, 0)),
            pl.BlockSpec((1, 768), lambda i: (0, 0)),
            pl.BlockSpec((1, 3, 768, 384), lambda i: (i, 0, 0, 0)),
            pl.BlockSpec((1, 384), lambda i: (0, 0)),
        ],
        out_specs=[
            pl.BlockSpec((256, 384), lambda i: (0, 0)),
            pl.BlockSpec((512, 384), lambda i: (0, 0)),
        ],
        scratch_shapes=[
            pltpu.VMEM((768, 256), BF16),
            pltpu.VMEM((768, 256), BF16),
            pltpu.VMEM((3, 2, 288, 768), BF16),
            pltpu.VMEM((512, 384), F32),
        ],
        cost_estimate=pl.CostEstimate(
            flops=2 * 512 * 9 * 384 * 768 + 6 * 256 * 768 * 768,
            transcendentals=0,
            bytes_accessed=9 << 20,
        ),
        name="convolve",
    )(idx, *cur, *nxt, tw, tb, sw, sb)


def per_device(queries, keys, values, tw, tb, sw, sb, cotangent):
    x_hi = lax.axis_index("space")
    x_lo = lax.axis_index("tm") // 2 % 2
    me = x_hi * 2 + x_lo
    around = [me ^ r for r in range(4)]
    slots = [(g % 2) * 2 + g // 2 for g in around]
    idx = jnp.stack(around + slots + [x_lo, x_hi]).astype(jnp.int32)

    flat = [a.reshape(TOK, 768) for a in (queries, keys, values)]
    piece = shape((3 * GROUP, TOK), BF16)
    packed = call(
        pack_body, [piece] * 4, [SM, VM, VM, VM], [pltpu.VMEM((3, 768, TOK), BF16)], name="pack"
    )(idx, *flat)
    got = [packed[0]] + [send(packed[r], flip_x(r)) for r in (1, 2, 3)]

    a_own, a_peer, b_own, b_peer = gradients(idx, cotangent.reshape(512, 384), sw, tw)

    q_own, kv_own = call(
        unpack_body,
        [shape((4, GROUP, TOK), BF16), shape((4, 2 * GROUP, TOK), BF16)],
        [SM] + [VM] * 4,
        name="unpack",
    )(idx, *got)
    qs = [q_own] + [send(q_own, turn_y(k)) for k in (1, 2, 3)]
    down1, up1 = send(kv_own, turn_z(1)), send(kv_own, turn_z(-1))
    down2, up2 = send(down1, turn_z(1)), send(up1, turn_z(-1))
    state = attend(qs, [kv_own, down1, up1], None, False)
    down3, up3 = send(down2, turn_z(1)), send(up2, turn_z(-1))
    state = attend(qs, [down2, up2], state, False)
    down4, up4 = send(down3[:2], turn_z(1)), send(up3[2:], turn_z(-1))
    state = attend(qs, [down3, up3], state, False)
    outs = attend(qs, [down4, up4], state, True)
    back = [outs[0]] + [send(outs[k], turn_y(-k)) for k in (1, 2, 3)]

    frame = shape((GROUP, 256), BF16)
    same, other = call(
        merge_body, [frame] * 2, [SM] + [VM] * 4, [pltpu.VMEM((2, GROUP, 256), BF16)], name="merge"
    )(idx, *back)
    cur = [same, send(other, flip_x(1)), send(same, flip_x(2)), send(other, flip_x(3))]
    nxt = [send(same if r & 1 else other, to_earlier_frame(r)) for r in range(4)]

    a_got = send(a_peer, flip_x(2))
    b_got = send(b_own, to_next_frame(0))
    c_got = send(b_peer, to_next_frame(2))
    grad = (
        a_own.astype(F32) + a_got.astype(F32) + b_got.astype(F32) + c_got.astype(F32)
    ).astype(BF16)

    att, refined = convolve(idx, cur, nxt, tw, tb.reshape(1, 768), sw, sb.reshape(1, 384))
    return (
        att.reshape(1, 16, 16, 384),
        refined.reshape(1, 2, 16, 16, 384),
        grad.reshape(1, 16, 16, 384),
    )


def solution(mesh):
    in_specs = (
        P("tm", "space", None, None),
        P("tm", "space", None, None),
        P("tm", "space", None, None),
        P(),
        P(),
        P(None, None, None, "space"),
        P("space"),
        P("tm", None, None, None, "space"),
    )
    out_specs = (
        P("tm", None, None, "space"),
        P("tm", None, None, None, "space"),
        P("tm", None, None, "space"),
    )
    return jax.shard_map(
        per_device, mesh=mesh, in_specs=in_specs, out_specs=out_specs, check_vma=False
    )
```
